256 devices in a mesh: rep: 4 (over y), fsdp: 64 (over x, z, core).
Axes of the slice: x: 4, y: 4, z: 8, core: 2. Of those that a mesh axis runs over, the one named last changes fastest.
Arguments:
- activations: bfloat16 [65536, 512], P(('rep', 'fsdp')), may hold values from -6 to 6
- output_grads: bfloat16 [65536, 8192], P(('rep', 'fsdp'))
- master: float32 [8192, 512], P('fsdp'), may hold values from -6 to 6
- first_moment: float32 [8192, 512], P('fsdp'), may hold values from -4 to 4
- second_moment: float32 [8192, 512], P('fsdp'), may hold values from 0.2 to 2
Outputs:
- new_master: float32 [8192, 512], P('fsdp')
- new_first: float32 [8192, 512], P('fsdp')
- new_second: float32 [8192, 512], P('fsdp')
- params: bfloat16 [8192, 512], replicated
The draws below stay inside these ranges and needn't reach their ends.
All inputs are finite; a program needn't handle non-finite values.
Results may differ from the reference program's by a relative error of at most 0.0004.
Values may be sent and summed in bfloat16 or wider, within the bound.
No kernel may reach another device: no remote copies, remote signals or barrier semaphores. Data moves between devices by JAX's collectives and lax.ppermute only.
A program may use at most 128 MiB of HBM per device.

```python
import math
import jax
import jax.numpy as jnp
from jax import lax

D = 8192
ROWS = 512
TOK_DEV = 256
LEVELS = 2
TOKENS = 16384
BATCH = 65536
N_REP = 4
N_FSDP = 64


def draw_activations(key, part):
    key_common, key_own = jax.random.split(jax.random.fold_in(key, 11))
    common = jax.random.normal(key_common, (TOKENS, ROWS), jnp.float32)
    own_part = jax.random.normal(key_own, (N_REP, TOKENS, ROWS), jnp.float32)
    share = 0.8
    mixed = share * common[None] + math.sqrt(1.0 - share * share) * own_part
    mixed = jnp.clip(mixed, -6.0, 6.0)
    return mixed.reshape(BATCH, ROWS).astype(jnp.bfloat16)


def draw_output_grads(key, part):
    key_common, key_own, key_gain, key_block = jax.random.split(jax.random.fold_in(key, 23), 4)
    common = jax.random.normal(key_common, (TOKENS, D), jnp.float32)
    own_part = jax.random.normal(key_own, (N_REP, TOKENS, D), jnp.float32)
    share = 0.7
    mixed = jnp.clip(share * common[None] + math.sqrt(1.0 - share * share) * own_part, -6.0, 6.0)
    device_place = (jnp.arange(TOKENS) // TOK_DEV).astype(jnp.float32)
    rising = 1.0 + 2.0 * device_place / max(N_FSDP - 1, 1)
    gains = jax.random.uniform(key_gain, (N_REP,), jnp.float32, 0.5, 2.0)
    block_count = N_FSDP * N_REP
    block_width = D // block_count
    block_logs = jax.random.uniform(key_block, (N_REP, block_count), jnp.float32, -0.8, 0.8)
    block_scale = jnp.repeat(jnp.exp(block_logs), block_width, axis=1)
    scaled = mixed * rising[None, :, None] * gains[:, None, None] * block_scale[:, None, :] / math.sqrt(TOKENS)
    return scaled.reshape(BATCH, D).astype(jnp.bfloat16)


def levels(stream_key, dims, cuts, low, largest):
    factor_of = 1.0
    for axis_at, blocks in cuts:
        heights = jax.random.uniform(jax.random.fold_in(jax.random.fold_in(stream_key, 6), axis_at), (blocks,), jnp.float32, low / len(cuts), largest / len(cuts))
        factor_of = factor_of * jnp.repeat(jnp.exp(heights), dims[axis_at] // blocks).reshape((-1,) + (1,) * (len(dims) - 1 - axis_at))
    return factor_of


def gaussian(rng, dims, deviation, bound, cuts=(), kind=jnp.bfloat16):
    level = levels(rng, dims, cuts, -0.22, 0.18) if cuts else 1.0
    array = jax.random.normal(rng, dims, jnp.float32) * deviation * level
    return jnp.minimum(jnp.maximum(array, -bound), bound).astype(kind)


def setup_inputs(seed: int = 0) -> dict:
    arg_keys = jax.random.split(jax.random.key(seed), 6)
    return {
        "activations": draw_activations(jax.random.fold_in(arg_keys[5], 71), 0),
        "output_grads": draw_output_grads(jax.random.fold_in(arg_keys[5], 71), 0),
        "master": gaussian(arg_keys[2], (D, ROWS), 0.5, 6.0, ((0, 64),), jnp.float32),
        "first_moment": gaussian(arg_keys[3], (D, ROWS), 0.3, 4.0, ((0, 64),), jnp.float32),
        "second_moment": jnp.clip(jnp.exp(math.log(2.0) - 2.3025851 * jax.random.uniform(arg_keys[4], (D, ROWS), jnp.float32) ** levels(arg_keys[4], (D, ROWS), ((0, 64),), -0.2, 0.2)), 0.2, 2.0),
    }


dot_epsilon = 1e-06
beta_one = 0.9
beta_two = 0.95
adam_epsilon = 1e-08
learn_rate = 0.02
decay_rate = 0.1
contract_first = (((0,), (0,)), ((), ()))

def adasum_pair(left_vec, right_vec):
    cross = jnp.sum(left_vec * right_vec)
    left_sq = jnp.sum(left_vec * left_vec)
    right_sq = jnp.sum(right_vec * right_vec)
    return (1.0 - cross / (2.0 * (left_sq + dot_epsilon))) * left_vec + (1.0 - cross / (2.0 * (right_sq + dot_epsilon))) * right_vec

def reference(activations, output_grads, master, first_moment, second_moment):
    group_acts = activations.reshape(N_REP, TOKENS, ROWS)
    group_outs = output_grads.reshape(N_REP, TOKENS, D)
    vectors = []
    for replica in range(N_REP):
        vectors.append(lax.dot_general(group_outs[replica], group_acts[replica], contract_first, preferred_element_type=jnp.float32))
    for level_index in range(LEVELS):
        vectors = [adasum_pair(vectors[2 * pair_index], vectors[2 * pair_index + 1]) for pair_index in range(len(vectors) // 2)]
    combined = vectors[0]
    correct_one = 1.0 - (beta_one ** 50) ** 2
    correct_two = 1.0 - (beta_two ** 50) ** 2
    new_first = beta_one * first_moment + (1.0 - beta_one) * combined
    new_second = beta_two * second_moment + (1.0 - beta_two) * combined * combined
    update = new_first / correct_one / (jnp.sqrt(new_second / correct_two) + adam_epsilon) + decay_rate * master
    new_master = master - learn_rate * update
    return (new_master, new_first, new_second, new_master.astype(jnp.bfloat16))
```

```python
import jax
import jax.numpy as jnp
from jax import lax
from jax.sharding import Mesh, PartitionSpec as P

dot_epsilon = 1e-06
beta_one = 0.9
beta_two = 0.95
adam_epsilon = 1e-08
learn_rate = 0.02
decay_rate = 0.1
contract_first = (((0,), (0,)), ((), ()))
GROUP = ("x", "z", "core")


def shifted(value, axis, step):
    size = lax.axis_size(axis)
    return lax.ppermute(value, axis, [(i, (i + step) % size) for i in range(size)])


def add_top(whole, part):
    rows = part.shape[0]
    return jnp.concatenate([whole[:rows] + part, whole[rows:]], axis=0)


def add_bottom(whole, part):
    rows = whole.shape[0] - part.shape[0]
    return jnp.concatenate([whole[:rows], whole[rows:] + part], axis=0)


def ring_reduce(chunk, axis):
    size = lax.axis_size(axis)
    half = size // 2
    far = chunk(half)
    rows = far.shape[0] // 2
    up = shifted(far[:rows], axis, 1)
    down = shifted(far[rows:], axis, -1)
    for reach in range(half - 1, 0, -1):
        if reach == half - 1:
            send_up, send_down = add_top(chunk(reach), up), add_bottom(chunk(-reach), down)
        else:
            send_up, send_down = chunk(reach) + up, chunk(-reach) + down
        up = shifted(send_up, axis, 1)
        down = shifted(send_down, axis, -1)
    return chunk(0) + up + down


def by_place(whole, axis):
    size = lax.axis_size(axis)
    place = lax.axis_index(axis)

    def chunk(step):
        return lax.dynamic_index_in_dim(whole, (place + step + size) % size, 0, keepdims=False)

    return chunk


def group_members(own):
    place = lax.axis_index("rep")
    below, above, across = shifted(own, "rep", 1), shifted(own, "rep", -1), shifted(own, "rep", 2)
    members = []
    for member in range(4):
        value = jnp.where(
            place == member,
            own,
            jnp.where(
                place == (member + 1) % 4, below, jnp.where(place == (member + 3) % 4, above, across)
            ),
        )
        members.append(value)
    return members


def pair_coefs(cross, left_sq, right_sq):
    return (
        1.0 - cross / (2.0 * (left_sq + dot_epsilon)),
        1.0 - cross / (2.0 * (right_sq + dot_epsilon)),
    )


def local(activations, output_grads, master, first_moment, second_moment):
    core = lax.axis_index("core")
    x_place = lax.axis_index("x")
    tokens, features = output_grads.shape
    width = activations.shape[1]
    rows = master.shape[0]
    half = width // 2
    with jax.named_scope("core_swap"):
        by_core = output_grads.reshape(tokens, features // (2 * rows), 2, rows)
        kept = jnp.where(core == 0, by_core[:, :, 0], by_core[:, :, 1]).reshape(tokens, features // 2)
        given = jnp.where(core == 0, by_core[:, :, 1], by_core[:, :, 0]).reshape(tokens, features // 2)
        grads = jnp.concatenate([kept, shifted(given, "core", 1)], axis=0)
        acts = jnp.concatenate([activations, shifted(activations, "core", 1)], axis=0)

    def product(grad_columns, act_columns):
        return lax.dot_general(
            grad_columns, act_columns, contract_first, preferred_element_type=jnp.float32
        )

    with jax.named_scope("reduce_b"):
        sums_b = product(grads, acts[:, half:]).reshape(4, 8, rows, half)
        sums_b = jnp.swapaxes(sums_b, 0, 1).reshape(8 * 4 * rows, half)
        sums_b = lax.psum_scatter(sums_b, "z", scatter_dimension=0, tiled=True)
    with jax.named_scope("reduce_a"):
        strip = features // 8

        def chunk_a(step):
            place = (x_place + step + 4) % 4
            return product(lax.dynamic_slice_in_dim(grads, place * strip, strip, 1), acts[:, :half])

        sums_a = ring_reduce(chunk_a, "x").reshape(8, rows, half)
        grad_a = ring_reduce(by_place(sums_a, "z"), "z")
    with jax.named_scope("reduce_b2"):
        grad_b = ring_reduce(by_place(sums_b.reshape(4, rows, half), "x"), "x")
    with jax.named_scope("members"):
        members_a = group_members(grad_a)
        members_b = group_members(grad_b)
        members = [jnp.concatenate(pair, axis=1) for pair in zip(members_a, members_b)]
    with jax.named_scope("gram"):
        pairs = [(i, j) for i in range(4) for j in range(i, 4)]
        sums = [jnp.sum(members[i] * members[j]) for i, j in pairs]
        row = jnp.concatenate([jnp.stack(sums), jnp.zeros((128 - len(sums),), jnp.float32)])
        everyone = lax.all_to_all(jnp.broadcast_to(row, (64, 1, 128)), GROUP, 0, 0)
        totals = jnp.sum(everyone, axis=(0, 1))
        gram = {pair: totals[index] for index, pair in enumerate(pairs)}
    with jax.named_scope("combine"):
        c0, c1 = pair_coefs(gram[0, 1], gram[0, 0], gram[1, 1])
        c2, c3 = pair_coefs(gram[2, 3], gram[2, 2], gram[3, 3])
        low_sq = c0 * c0 * gram[0, 0] + 2.0 * c0 * c1 * gram[0, 1] + c1 * c1 * gram[1, 1]
        high_sq = c2 * c2 * gram[2, 2] + 2.0 * c2 * c3 * gram[2, 3] + c3 * c3 * gram[3, 3]
        cross = c0 * (c2 * gram[0, 2] + c3 * gram[0, 3]) + c1 * (c2 * gram[1, 2] + c3 * gram[1, 3])
        low, high = pair_coefs(cross, jnp.maximum(low_sq, 0.0), jnp.maximum(high_sq, 0.0))
        combined = low * (c0 * members[0] + c1 * members[1]) + high * (
            c2 * members[2] + c3 * members[3]
        )
    with jax.named_scope("adamw"):
        correct_one = 1.0 - (beta_one**50) ** 2
        correct_two = 1.0 - (beta_two**50) ** 2
        new_first = beta_one * first_moment + (1.0 - beta_one) * combined
        new_second = beta_two * second_moment + (1.0 - beta_two) * combined * combined
        update = (
            new_first / correct_one / (jnp.sqrt(new_second / correct_two) + adam_epsilon)
            + decay_rate * master
        )
        new_master = master - learn_rate * update
    with jax.named_scope("params"):
        params = lax.all_gather(new_master.astype(jnp.bfloat16), GROUP, axis=0, tiled=True)
    return (new_master, new_first, new_second, params)


def solution(mesh):
    fine = Mesh(mesh.devices.reshape(4, 4, 8, 2), ("rep",) + GROUP)
    everyone = P(("rep",) + GROUP, None)
    block = P(GROUP, None)
    return jax.shard_map(
        local,
        mesh=fine,
        in_specs=(everyone, everyone, block, block, block),
        out_specs=(block, block, block, P()),
        check_vma=False,
    )
```

```python
import functools

import jax
import jax.numpy as jnp
from jax import lax
from jax.experimental import pallas as pl
from jax.experimental.pallas import tpu as pltpu
from jax.sharding import Mesh, PartitionSpec as P

dot_epsilon = 1e-06
beta_one = 0.9
beta_two = 0.95
adam_epsilon = 1e-08
learn_rate = 0.02
decay_rate = 0.1
contract_first = (((0,), (0,)), ((), ()))
GROUP = ("x", "z", "core")
ROWS_A = 80


def shifted(value, axis, step):
    size = lax.axis_size(axis)
    return lax.ppermute(value, axis, [(i, (i + step) % size) for i in range(size)])


def add_top(whole, part):
    rows = part.shape[0]
    return jnp.concatenate([whole[:rows] + part, whole[rows:]], axis=0)


def add_bottom(whole, part):
    rows = whole.shape[0] - part.shape[0]
    return jnp.concatenate([whole[:rows], whole[rows:] + part], axis=0)


def ring_reduce(chunk, axis):
    size = lax.axis_size(axis)
    half = size // 2
    far = chunk(half)
    rows = far.shape[0] // 2
    up = shifted(far[:rows], axis, 1)
    down = shifted(far[rows:], axis, -1)
    for reach in range(half - 1, 0, -1):
        if reach == half - 1:
            send_up, send_down = add_top(chunk(reach), up), add_bottom(chunk(-reach), down)
        else:
            send_up, send_down = chunk(reach) + up, chunk(-reach) + down
        up = shifted(send_up, axis, 1)
        down = shifted(send_down, axis, -1)
    return chunk(0) + up + down


def by_place(whole, axis):
    size = lax.axis_size(axis)
    place = lax.axis_index(axis)

    def chunk(step):
        return lax.dynamic_index_in_dim(whole, (place + step + size) % size, 0, keepdims=False)

    return chunk


def neighbours(own, axis):
    return [own, shifted(own, axis, -1), shifted(own, axis, 2), shifted(own, axis, 1)]


def in_vmem(count):
    return [pl.BlockSpec(memory_space=pltpu.VMEM)] * count


def split_kernel(block, grads_ref, kept_ref, given_ref):
    low = lax.axis_index("core") == 0
    for z in range(8):
        for x in range(4):
            first = grads_ref[:, pl.ds((x * 16 + z * 2) * block, block)]
            second = grads_ref[:, pl.ds((x * 16 + z * 2 + 1) * block, block)]
            place = pl.ds((z * 4 + x) * block, block)
            kept_ref[:, place] = jnp.where(low, first, second)
            given_ref[:, place] = jnp.where(low, second, first)


def split_columns(grads, block):
    tokens, features = grads.shape
    step = tokens // 4
    half = jax.ShapeDtypeStruct((tokens, features // 2), grads.dtype)
    half_spec = pl.BlockSpec((step, features // 2), lambda i: (i, 0))
    return pl.pallas_call(
        lambda *refs: split_kernel(block, *refs),
        grid=(4,),
        in_specs=[pl.BlockSpec((step, features), lambda i: (i, 0))],
        out_specs=[half_spec, half_spec],
        out_shape=[half, half],
        name="split_columns",
    )(grads)


PAIRS = [(i, j) for i in range(4) for j in range(i, 4)]


def gram_kernel(a0, a1, a2, a3, b0, b1, b2, b3, members_ref, rows_ref):
    place = lax.axis_index("rep")
    half = a0.shape[1]
    for step, (left, right) in enumerate(zip((a0, a1, a2, a3), (b0, b1, b2, b3))):
        member = lax.rem(place + step, 4)
        members_ref[member, :, :half] = left[...]
        members_ref[member, :, half:] = right[...]
    lane = lax.broadcasted_iota(jnp.int32, (1, 128), 1)
    row = jnp.zeros((1, 128), jnp.float32)
    for index, (i, j) in enumerate(PAIRS):
        row = jnp.where(lane == index, jnp.sum(members_ref[i] * members_ref[j]), row)
    rows_ref[...] = jnp.broadcast_to(row[None], rows_ref.shape)


def gram_rows(pieces_a, pieces_b):
    rows, half = pieces_a[0].shape
    return pl.pallas_call(
        gram_kernel,
        in_specs=in_vmem(8),
        out_specs=in_vmem(2),
        out_shape=[
            jax.ShapeDtypeStruct((4, rows, 2 * half), jnp.float32),
            jax.ShapeDtypeStruct((64, 1, 128), jnp.float32),
        ],
        name="gram_rows",
    )(*pieces_a, *pieces_b)


def pair_coefs(cross, left_sq, right_sq):
    return (
        1.0 - cross / (2.0 * (left_sq + dot_epsilon)),
        1.0 - cross / (2.0 * (right_sq + dot_epsilon)),
    )


def update_kernel(
    everyone_ref, members_ref, master_ref, first_ref, second_ref,
    new_master_ref, new_first_ref, new_second_ref, params_a_ref, params_b_ref,
):
    totals = jnp.sum(everyone_ref[...], axis=0)
    gram = {pair: totals[:, index : index + 1] for index, pair in enumerate(PAIRS)}
    c0, c1 = pair_coefs(gram[0, 1], gram[0, 0], gram[1, 1])
    c2, c3 = pair_coefs(gram[2, 3], gram[2, 2], gram[3, 3])
    low_sq = c0 * c0 * gram[0, 0] + 2.0 * c0 * c1 * gram[0, 1] + c1 * c1 * gram[1, 1]
    high_sq = c2 * c2 * gram[2, 2] + 2.0 * c2 * c3 * gram[2, 3] + c3 * c3 * gram[3, 3]
    cross = c0 * (c2 * gram[0, 2] + c3 * gram[0, 3]) + c1 * (c2 * gram[1, 2] + c3 * gram[1, 3])
    low, high = pair_coefs(cross, jnp.maximum(low_sq, 0.0), jnp.maximum(high_sq, 0.0))
    combined = low * (c0 * members_ref[0] + c1 * members_ref[1]) + high * (
        c2 * members_ref[2] + c3 * members_ref[3]
    )
    correct_one = 1.0 - (beta_one**50) ** 2
    correct_two = 1.0 - (beta_two**50) ** 2
    new_first = beta_one * first_ref[...] + (1.0 - beta_one) * combined
    new_second = beta_two * second_ref[...] + (1.0 - beta_two) * combined * combined
    master = master_ref[...]
    update = (
        new_first / correct_one / (jnp.sqrt(new_second / correct_two) + adam_epsilon)
        + decay_rate * master
    )
    new_master = master - learn_rate * update
    new_first_ref[...] = new_first
    new_second_ref[...] = new_second
    new_master_ref[...] = new_master
    half = params_a_ref.shape[0]
    params_a_ref[...] = new_master[:half].astype(jnp.bfloat16)
    params_b_ref[...] = new_master[half:].astype(jnp.bfloat16)


def updated(everyone, members, master, first, second):
    rows, width = master.shape
    whole = jax.ShapeDtypeStruct((rows, width), jnp.float32)
    part_a = jax.ShapeDtypeStruct((ROWS_A, width), jnp.bfloat16)
    part_b = jax.ShapeDtypeStruct((rows - ROWS_A, width), jnp.bfloat16)
    return pl.pallas_call(
        update_kernel,
        in_specs=in_vmem(5),
        out_specs=in_vmem(5),
        out_shape=[whole, whole, whole, part_a, part_b],
        name="updated",
    )(everyone, members, master, first, second)


def place_kernel(size_a, order, *refs):
    pieces, out, sems = refs[: len(order)], refs[-2], refs[-1]
    core, x_place = lax.axis_index("core"), lax.axis_index("x")
    copies = []
    for piece, (colour, side, step) in zip(pieces, order):
        owner = core if side == 0 else 1 - core
        if colour == 0:
            for x in range(4):
                copies.append((piece.at[:, x], out.at[x, :, owner, pl.ds(0, size_a)]))
        else:
            x = lax.rem(x_place + step, 4)
            rows = piece.shape[1]
            copies.append((piece, out.at[x, :, owner, pl.ds(size_a, rows)]))
    started = [
        pltpu.make_async_copy(source, target, sems.at[index])
        for index, (source, target) in enumerate(copies)
    ]
    for copy in started:
        copy.start()
    for copy in started:
        copy.wait()


def placed(out, pieces, order, shape, size_a):
    first = out is None
    return pl.pallas_call(
        functools.partial(place_kernel, size_a, order),
        in_specs=in_vmem(len(pieces)) + ([] if first else [pl.BlockSpec(memory_space=pl.ANY)]),
        out_specs=pl.BlockSpec(memory_space=pl.ANY),
        out_shape=jax.ShapeDtypeStruct(shape, jnp.bfloat16),
        scratch_shapes=[pltpu.SemaphoreType.DMA((len(pieces) + 3,))],
        input_output_aliases={} if first else {len(pieces): 0},
        compiler_params=pltpu.CompilerParams(vmem_limit_bytes=32 * 1024 * 1024),
        name="placed",
    )(*pieces, *([] if first else [out]))


def gathered(params_a, params_b):
    rows_a, width = params_a.shape
    rows_b = params_b.shape[0]
    x_place = lax.axis_index("x")
    near = neighbours(params_a, "x")
    ordered = []
    for x in range(4):
        value = near[0]
        for step in range(1, 4):
            value = jnp.where((x_place + step) % 4 == x, near[step], value)
        ordered.append(value)
    line = jnp.concatenate(ordered, axis=0)
    line, params_b = lax.optimization_barrier((line, params_b))
    own_a = lax.all_gather(line, "z", axis=0, tiled=True).reshape(8, 4, rows_a, width)
    column = lax.all_to_all(jnp.broadcast_to(params_b[None], (8, rows_b, width)), "z", 0, 0)
    own_b = neighbours(column, "x")
    own_a, *own_b = lax.optimization_barrier((own_a, *own_b))
    other_b = [shifted(piece, "core", 1) for piece in own_b]
    other_a = shifted(own_a, "core", 1)
    order = [(1, 0, step) for step in range(4)] + [(1, 1, step) for step in range(4)] + [(0, 0, 0)]
    shape = (4, 8, 2, rows_a + rows_b, width)
    out = placed(None, [*own_b, *other_b, own_a], order, shape, rows_a)
    out = placed(out, [other_a], [(0, 1, 0)], shape, rows_a)
    return out.reshape(-1, width)


def local(activations, output_grads, master, first_moment, second_moment):
    width = activations.shape[1]
    rows = master.shape[0]
    half = width // 2
    with jax.named_scope("core_swap"):
        kept, given = split_columns(output_grads, rows)
        grads = jnp.concatenate([kept, shifted(given, "core", 1)], axis=0)
        acts = jnp.concatenate([activations, shifted(activations, "core", 1)], axis=0)

    def product(act_columns):
        return lax.dot_general(
            grads, act_columns, contract_first, preferred_element_type=jnp.float32
        )

    with jax.named_scope("reduce_b"):
        sums_b = lax.psum_scatter(
            product(acts[:, half:]), "z", scatter_dimension=0, tiled=True
        )
    with jax.named_scope("reduce_a"):
        sums_a = product(acts[:, :half]).reshape(8, 4, rows, half)
        x_place = lax.axis_index("x")

        def chunk_a(step):
            return lax.dynamic_index_in_dim(sums_a, (x_place + step + 4) % 4, 1, keepdims=False)

        sums_a = ring_reduce(chunk_a, "x")
        grad_a = ring_reduce(by_place(sums_a, "z"), "z")
    with jax.named_scope("reduce_b2"):
        grad_b = ring_reduce(by_place(sums_b.reshape(4, rows, half), "x"), "x")
    with jax.named_scope("members"):
        members, row = gram_rows(neighbours(grad_a, "rep"), neighbours(grad_b, "rep"))
    with jax.named_scope("gram"):
        everyone = lax.all_to_all(row, GROUP, 0, 0)
    with jax.named_scope("adamw"):
        new_master, new_first, new_second, params_a, params_b = updated(
            everyone, members, master, first_moment, second_moment
        )
    with jax.named_scope("params"):
        params = gathered(params_a, params_b)
    return (new_master, new_first, new_second, params)


def solution(mesh):
    fine = Mesh(mesh.devices.reshape(4, 4, 8, 2), ("rep",) + GROUP)
    everyone = P(("rep",) + GROUP, None)
    block = P(GROUP, None)
    return jax.shard_map(
        local,
        mesh=fine,
        in_specs=(everyone, everyone, block, block, block),
        out_specs=(block, block, block, P()),
        check_vma=False,
    )
```

```python
import functools

import jax
import jax.numpy as jnp
from jax import lax
from jax.experimental import pallas as pl
from jax.experimental.pallas import tpu as pltpu
from jax.sharding import Mesh, PartitionSpec as P

dot_epsilon = 1e-06
beta_one = 0.9
beta_two = 0.95
adam_epsilon = 1e-08
learn_rate = 0.02
decay_rate = 0.1
contract_first = (((0,), (0,)), ((), ()))
GROUP = ("x", "z", "core")
ROWS_A = 80


def shifted(value, axis, step):
    size = lax.axis_size(axis)
    return lax.ppermute(value, axis, [(i, (i + step) % size) for i in range(size)])


def add_top(whole, part):
    rows = part.shape[0]
    return jnp.concatenate([whole[:rows] + part, whole[rows:]], axis=0)


def add_bottom(whole, part):
    rows = whole.shape[0] - part.shape[0]
    return jnp.concatenate([whole[:rows], whole[rows:] + part], axis=0)


def ring_reduce(chunk, axis, gates):
    size = lax.axis_size(axis)
    half = size // 2
    far = chunk(half)
    rows = far.shape[0] // 2
    up = shifted(far[:rows], axis, 1)
    down = shifted(far[rows:], axis, -1)
    for reach in range(half - 1, 0, -1):
        if reach == half - 1:
            send_up, send_down = add_top(chunk(reach), up), add_bottom(chunk(-reach), down)
        else:
            send_up, send_down = chunk(reach) + up, chunk(-reach) + down
        if reach in gates:
            send_up, send_down = gates[reach](send_up, send_down)
        up = shifted(send_up, axis, 1)
        down = shifted(send_down, axis, -1)
    return chunk(0) + up + down


def by_place(whole, axis):
    size = lax.axis_size(axis)
    place = lax.axis_index(axis)

    def chunk(step):
        return lax.dynamic_index_in_dim(whole, (place + step + size) % size, 0, keepdims=False)

    return chunk


def neighbours(own, axis):
    return [own, shifted(own, axis, -1), shifted(own, axis, 2), shifted(own, axis, 1)]


def in_vmem(count):
    return [pl.BlockSpec(memory_space=pltpu.VMEM)] * count


def split_kernel(block, colour, grads_ref, kept_ref, given_ref):
    low = lax.axis_index("core") == 0
    half = block // 2
    lane = lax.broadcasted_iota(jnp.int32, (grads_ref.shape[0], block), 1)

    def swapped_halves(value):
        return pltpu.roll(value.astype(jnp.float32), half, 1).astype(value.dtype)

    def pair(left, right):
        if colour == "A":
            return jnp.where(lane < half, left, swapped_halves(right))
        return jnp.where(lane < half, swapped_halves(left), right)

    def block_at(x, z, core):
        return grads_ref[:, pl.ds((x * 16 + z * 2 + core) * block, block)]

    if colour == "A":
        order = [(x, z) for x in range(4) for z in range(8)]
    else:
        order = [(x, z) for z in range(8) for x in range(4)]
    for index in range(0, len(order), 2):
        sides = [pair(*(block_at(*place, core) for place in order[index : index + 2])) for core in range(2)]
        where = pl.ds(index * half, block)
        kept_ref[:, where] = jnp.where(low, sides[0], sides[1])
        given_ref[:, where] = jnp.where(low, sides[1], sides[0])


def split_columns(grads, block, colour):
    tokens, features = grads.shape
    step = tokens // 4
    part = jax.ShapeDtypeStruct((tokens, features // 4), grads.dtype)
    part_spec = pl.BlockSpec((step, features // 4), lambda i: (i, 0))
    return pl.pallas_call(
        functools.partial(split_kernel, block, colour),
        grid=(4,),
        in_specs=[pl.BlockSpec((step, features), lambda i: (i, 0))],
        out_specs=[part_spec, part_spec],
        out_shape=[part, part],
        name="split_columns",
    )(grads)


PAIRS = [(i, j) for i in range(4) for j in range(i, 4)]


def gram_kernel(a0, a1, a2, a3, b0, b1, b2, b3, members_ref, rows_ref):
    place = lax.axis_index("rep")
    half = a0.shape[0]
    for step, (left, right) in enumerate(zip((a0, a1, a2, a3), (b0, b1, b2, b3))):
        member = lax.rem(place + step, 4)
        members_ref[member, :half] = left[...]
        members_ref[member, half:] = right[...]
    lane = lax.broadcasted_iota(jnp.int32, (1, 128), 1)
    row = jnp.zeros((1, 128), jnp.float32)
    for index, (i, j) in enumerate(PAIRS):
        row = jnp.where(lane == index, jnp.sum(members_ref[i] * members_ref[j]), row)
    rows_ref[...] = jnp.broadcast_to(row[None], rows_ref.shape)


def gram_rows(pieces_a, pieces_b):
    half, width = pieces_a[0].shape
    return pl.pallas_call(
        gram_kernel,
        in_specs=in_vmem(8),
        out_specs=in_vmem(2),
        out_shape=[
            jax.ShapeDtypeStruct((4, 2 * half, width), jnp.float32),
            jax.ShapeDtypeStruct((64, 1, 128), jnp.float32),
        ],
        name="gram_rows",
    )(*pieces_a, *pieces_b)


def pair_coefs(cross, left_sq, right_sq):
    return (
        1.0 - cross / (2.0 * (left_sq + dot_epsilon)),
        1.0 - cross / (2.0 * (right_sq + dot_epsilon)),
    )


def update_kernel(
    everyone_ref, members_ref, master_ref, first_ref, second_ref,
    new_master_ref, new_first_ref, new_second_ref, params_a_ref, params_b_ref,
):
    totals = jnp.sum(everyone_ref[...], axis=0)
    gram = {pair: totals[:, index : index + 1] for index, pair in enumerate(PAIRS)}
    c0, c1 = pair_coefs(gram[0, 1], gram[0, 0], gram[1, 1])
    c2, c3 = pair_coefs(gram[2, 3], gram[2, 2], gram[3, 3])
    low_sq = c0 * c0 * gram[0, 0] + 2.0 * c0 * c1 * gram[0, 1] + c1 * c1 * gram[1, 1]
    high_sq = c2 * c2 * gram[2, 2] + 2.0 * c2 * c3 * gram[2, 3] + c3 * c3 * gram[3, 3]
    cross = c0 * (c2 * gram[0, 2] + c3 * gram[0, 3]) + c1 * (c2 * gram[1, 2] + c3 * gram[1, 3])
    low, high = pair_coefs(cross, jnp.maximum(low_sq, 0.0), jnp.maximum(high_sq, 0.0))
    combined = low * (c0 * members_ref[0] + c1 * members_ref[1]) + high * (
        c2 * members_ref[2] + c3 * members_ref[3]
    )
    correct_one = 1.0 - (beta_one**50) ** 2
    correct_two = 1.0 - (beta_two**50) ** 2
    new_first = beta_one * first_ref[...] + (1.0 - beta_one) * combined
    new_second = beta_two * second_ref[...] + (1.0 - beta_two) * combined * combined
    master = master_ref[...]
    update = (
        new_first / correct_one / (jnp.sqrt(new_second / correct_two) + adam_epsilon)
        + decay_rate * master
    )
    new_master = master - learn_rate * update
    new_first_ref[...] = new_first
    new_second_ref[...] = new_second
    new_master_ref[...] = new_master
    half = params_a_ref.shape[0]
    params_a_ref[...] = new_master[:half].astype(jnp.bfloat16)
    params_b_ref[...] = new_master[half:].astype(jnp.bfloat16)


def updated(everyone, members, master, first, second):
    rows, width = master.shape
    whole = jax.ShapeDtypeStruct((rows, width), jnp.float32)
    part_a = jax.ShapeDtypeStruct((ROWS_A, width), jnp.bfloat16)
    part_b = jax.ShapeDtypeStruct((rows - ROWS_A, width), jnp.bfloat16)
    return pl.pallas_call(
        update_kernel,
        in_specs=in_vmem(5),
        out_specs=in_vmem(5),
        out_shape=[whole, whole, whole, part_a, part_b],
        name="updated",
    )(everyone, members, master, first, second)


def place_kernel(size_a, order, *refs):
    pieces, out, sems = refs[: len(order)], refs[-2], refs[-1]
    core, x_place = lax.axis_index("core"), lax.axis_index("x")
    copies = []
    for piece, (colour, side, step) in zip(pieces, order):
        owner = core if side == 0 else 1 - core
        if colour == 0:
            for up in range(4):
                x = lax.rem(x_place + up, 4)
                copies.append((piece.at[:, up], out.at[x, :, owner, pl.ds(0, size_a)]))
        else:
            x = lax.rem(x_place + step, 4)
            rows = piece.shape[1]
            copies.append((piece, out.at[x, :, owner, pl.ds(size_a, rows)]))
    started = [
        pltpu.make_async_copy(source, target, sems.at[index])
        for index, (source, target) in enumerate(copies)
    ]
    for copy in started:
        copy.start()
    for copy in started:
        copy.wait()


def placed(out, pieces, order, shape, size_a):
    first = out is None
    return pl.pallas_call(
        functools.partial(place_kernel, size_a, order),
        in_specs=in_vmem(len(pieces)) + ([] if first else [pl.BlockSpec(memory_space=pl.ANY)]),
        out_specs=pl.BlockSpec(memory_space=pl.ANY),
        out_shape=jax.ShapeDtypeStruct(shape, jnp.bfloat16),
        scratch_shapes=[pltpu.SemaphoreType.DMA((len(pieces) + 3,))],
        input_output_aliases={} if first else {len(pieces): 0},
        compiler_params=pltpu.CompilerParams(vmem_limit_bytes=32 * 1024 * 1024),
        name="placed",
    )(*pieces, *([] if first else [out]))


def gathered(params_a, params_b):
    rows_a, width = params_a.shape
    rows_b = params_b.shape[0]
    line = jnp.concatenate(neighbours(params_a, "x"), axis=0)
    line, params_b = lax.optimization_barrier((line, params_b))
    own_a = lax.all_gather(line, "z", axis=0, tiled=True).reshape(8, 4, rows_a, width)
    column = lax.all_to_all(jnp.broadcast_to(params_b[None], (8, rows_b, width)), "z", 0, 0)
    own_b = neighbours(column, "x")
    other_b = [shifted(piece, "core", 1) for piece in own_b]
    order = [(1, side, step) for side in range(2) for step in range(4)]
    shape = (4, 8, 2, rows_a + rows_b, width)
    out = placed(None, [*own_b, *other_b], order, shape, rows_a)
    own_a, out = lax.optimization_barrier((own_a, out))
    other_a = shifted(own_a, "core", 1)
    out = placed(out, [own_a], [(0, 0, 0)], shape, rows_a)
    out = placed(out, [other_a], [(0, 1, 0)], shape, rows_a)
    return out.reshape(-1, width)


def local(activations, output_grads, master, first_moment, second_moment):
    width = activations.shape[1]
    rows = master.shape[0]
    half = rows // 2
    x_place = lax.axis_index("x")

    def product(grad_columns, act_rows):
        return lax.dot_general(
            grad_columns, act_rows, contract_first, preferred_element_type=jnp.float32
        )

    def pair_up_parts(own, given):
        return jnp.concatenate([own, shifted(given, "core", 1)], axis=0)

    def pair_up(own):
        return pair_up_parts(own, own)

    with jax.named_scope("core_swap"):
        near_acts = neighbours(activations, "x")
        kept_b, given_b = split_columns(output_grads, rows, "B")
        own_acts = pair_up(activations)
        grads_b = pair_up_parts(kept_b, given_b)
        kept_a, given_a = split_columns(output_grads, rows, "A")
        given_a, own_acts, near_acts[1], near_acts[3] = lax.optimization_barrier(
            (given_a, own_acts, near_acts[1], near_acts[3])
        )
        grads_a = pair_up_parts(kept_a, given_a)
        line_acts = [own_acts] + [pair_up(part) for part in near_acts[1:]]
    with jax.named_scope("reduce_b"):
        sums_b = product(grads_b, line_acts[0])
        sums_b = lax.psum_scatter(sums_b, "z", scatter_dimension=0, tiled=True)
        chunk_b = by_place(sums_b.reshape(4, half, width), "x")
        chunks_b = [chunk_b(step) for step in range(4)]
    with jax.named_scope("reduce_a"):
        strip = 8 * half

        def columns_of(step):
            return lax.dynamic_slice_in_dim(grads_a, (x_place + step) % 4 * strip, strip, 1)

        line_grads = [
            columns_of(0),
            shifted(columns_of(3), "x", -1),
            shifted(columns_of(2), "x", 2),
            shifted(columns_of(1), "x", 1),
        ]
        sums_a = sum(product(part, acts) for part, acts in zip(line_grads, line_acts))

        exchanged_b = []

        def start_b(send_up, send_down):
            send_up, send_down, *chunks = lax.optimization_barrier(
                (send_up, send_down, *chunks_b[1:])
            )
            with jax.named_scope("reduce_b2"):
                near = shifted(chunks[2], "x", -1) + shifted(chunks[0], "x", 1)
                exchanged_b.append(chunks_b[0] + (near + shifted(chunks[1], "x", 2)))
            return send_up, send_down

        gates = {2: start_b}
        grad_a = ring_reduce(by_place(sums_a.reshape(8, half, width), "z"), "z", gates)
    with jax.named_scope("members"):
        members, row = gram_rows(neighbours(grad_a, "rep"), neighbours(exchanged_b.pop(), "rep"))
    with jax.named_scope("gram"):
        everyone = lax.all_to_all(row, GROUP, 0, 0)
    with jax.named_scope("adamw"):
        new_master, new_first, new_second, params_a, params_b = updated(
            everyone, members, master, first_moment, second_moment
        )
    with jax.named_scope("params"):
        params = gathered(params_a, params_b)
    return (new_master, new_first, new_second, params)


def solution(mesh):
    fine = Mesh(mesh.devices.reshape(4, 4, 8, 2), ("rep",) + GROUP)
    everyone = P(("rep",) + GROUP, None)
    block = P(GROUP, None)
    return jax.shard_map(
        local,
        mesh=fine,
        in_specs=(everyone, everyone, block, block, block),
        out_specs=(block, block, block, P()),
        check_vma=False,
    )
```

```python
import functools

import jax
import jax.numpy as jnp
from jax import lax
from jax.experimental import pallas as pl
from jax.experimental.pallas import tpu as pltpu
from jax.sharding import Mesh, PartitionSpec as P

dot_epsilon = 1e-06
beta_one = 0.9
beta_two = 0.95
adam_epsilon = 1e-08
learn_rate = 0.02
decay_rate = 0.1
contract_first = (((0,), (0,)), ((), ()))
GROUP = ("x", "z", "core")
ROWS_A = 80


def shifted(value, axis, step):
    size = lax.axis_size(axis)
    return lax.ppermute(value, axis, [(i, (i + step) % size) for i in range(size)])


def add_top(whole, part):
    rows = part.shape[0]
    return jnp.concatenate([whole[:rows] + part, whole[rows:]], axis=0)


def add_bottom(whole, part):
    rows = whole.shape[0] - part.shape[0]
    return jnp.concatenate([whole[:rows], whole[rows:] + part], axis=0)


def ring_reduce(chunk, axis, gates):
    size = lax.axis_size(axis)
    half = size // 2
    far = chunk(half)
    rows = far.shape[0] // 2
    up = shifted(far[:rows], axis, 1)
    down = shifted(far[rows:], axis, -1)
    for reach in range(half - 1, 0, -1):
        if reach == half - 1:
            send_up, send_down = add_top(chunk(reach), up), add_bottom(chunk(-reach), down)
        else:
            send_up, send_down = chunk(reach) + up, chunk(-reach) + down
        if reach in gates:
            send_up, send_down = gates[reach](send_up, send_down)
        up = shifted(send_up, axis, 1)
        down = shifted(send_down, axis, -1)
    return chunk(0) + up + down


def by_place(whole, axis, flip):
    size = lax.axis_size(axis)
    place = lax.axis_index(axis)

    def chunk(step):
        return lax.dynamic_index_in_dim(whole, ((place + step + size) % size) ^ flip, 0, keepdims=False)

    return chunk


def neighbours(own, axis):
    return [own, shifted(own, axis, -1), shifted(own, axis, 2), shifted(own, axis, 1)]


def in_vmem(count):
    return [pl.BlockSpec(memory_space=pltpu.VMEM)] * count


def split_kernel(block, colour, *refs):
    *strips, kept_ref, given_ref = refs
    core = lax.axis_index("core")
    half = block // 2
    first_lanes = lax.broadcasted_iota(jnp.int32, (kept_ref.shape[0], block), 1) < half
    if colour == "A":
        order = [(x, slot ^ (x & 1)) for x in range(4) for slot in range(8)]
    else:
        order = [(slot ^ (z & 1) ^ 1, z) for z in range(8) for slot in range(4)]
    for out_ref, side in ((given_ref, 1 - core), (kept_ref, core)):
        for index in range(0, len(order), 2):
            left, right = (
                strips[x * 2 + z // 4][
                    :, pl.ds(pl.multiple_of((z % 4 * 2 + side) * block, block), block)
                ]
                for x, z in order[index : index + 2]
            )
            out_ref[:, pl.ds(index * half, block)] = jnp.where(first_lanes, left, right)


def split_columns(grads, block, colour):
    tokens, features = grads.shape
    step = tokens // 2
    part = jax.ShapeDtypeStruct((tokens, features // 4), grads.dtype)
    part_spec = pl.BlockSpec((step, features // 4), lambda i: (i, 0))
    return pl.pallas_call(
        functools.partial(split_kernel, block, colour),
        grid=(2,),
        in_specs=[
            pl.BlockSpec((step, features // 8), functools.partial(lambda strip, i: (i, strip), strip))
            for strip in range(8)
        ],
        out_specs=[part_spec, part_spec],
        out_shape=[part, part],
        name="split_columns",
    )(*[grads] * 8)


PAIRS = [(i, j) for i in range(4) for j in range(i, 4)]


def gram_kernel(a0, a1, a2, a3, b0, b1, b2, b3, members_ref, rows_ref):
    place = lax.axis_index("rep")
    half = a0.shape[0]
    odd = lax.rem(lax.axis_index("x") + lax.axis_index("z"), 2)
    for step, (left, right) in enumerate(zip((a0, a1, a2, a3), (b0, b1, b2, b3))):
        member = lax.rem(place + step, 4)
        members_ref[member, pl.ds(pl.multiple_of(odd * half, half), half)] = left[...]
        members_ref[member, pl.ds(pl.multiple_of((1 - odd) * half, half), half)] = right[...]
    lane = lax.broadcasted_iota(jnp.int32, (1, 128), 1)
    row = jnp.zeros((1, 128), jnp.float32)
    for index, (i, j) in enumerate(PAIRS):
        row = jnp.where(lane == index, jnp.sum(members_ref[i] * members_ref[j]), row)
    rows_ref[...] = jnp.broadcast_to(row[None], rows_ref.shape)


def gram_rows(pieces_a, pieces_b):
    half, width = pieces_a[0].shape
    return pl.pallas_call(
        gram_kernel,
        in_specs=in_vmem(8),
        out_specs=in_vmem(2),
        out_shape=[
            jax.ShapeDtypeStruct((4, 2 * half, width), jnp.float32),
            jax.ShapeDtypeStruct((64, 1, 128), jnp.float32),
        ],
        name="gram_rows",
    )(*pieces_a, *pieces_b)


def pair_coefs(cross, left_sq, right_sq):
    return (
        1.0 - cross / (2.0 * (left_sq + dot_epsilon)),
        1.0 - cross / (2.0 * (right_sq + dot_epsilon)),
    )


def update_kernel(
    everyone_ref, members_ref, master_ref, first_ref, second_ref,
    new_master_ref, new_first_ref, new_second_ref, params_a_ref, params_b_ref,
):
    totals = jnp.sum(everyone_ref[...], axis=0)
    gram = {pair: totals[:, index : index + 1] for index, pair in enumerate(PAIRS)}
    c0, c1 = pair_coefs(gram[0, 1], gram[0, 0], gram[1, 1])
    c2, c3 = pair_coefs(gram[2, 3], gram[2, 2], gram[3, 3])
    low_sq = c0 * c0 * gram[0, 0] + 2.0 * c0 * c1 * gram[0, 1] + c1 * c1 * gram[1, 1]
    high_sq = c2 * c2 * gram[2, 2] + 2.0 * c2 * c3 * gram[2, 3] + c3 * c3 * gram[3, 3]
    cross = c0 * (c2 * gram[0, 2] + c3 * gram[0, 3]) + c1 * (c2 * gram[1, 2] + c3 * gram[1, 3])
    low, high = pair_coefs(cross, jnp.maximum(low_sq, 0.0), jnp.maximum(high_sq, 0.0))
    combined = low * (c0 * members_ref[0] + c1 * members_ref[1]) + high * (
        c2 * members_ref[2] + c3 * members_ref[3]
    )
    correct_one = 1.0 - (beta_one**50) ** 2
    correct_two = 1.0 - (beta_two**50) ** 2
    new_first = beta_one * first_ref[...] + (1.0 - beta_one) * combined
    new_second = beta_two * second_ref[...] + (1.0 - beta_two) * combined * combined
    master = master_ref[...]
    update = (
        new_first / correct_one / (jnp.sqrt(new_second / correct_two) + adam_epsilon)
        + decay_rate * master
    )
    new_master = master - learn_rate * update
    new_first_ref[...] = new_first
    new_second_ref[...] = new_second
    new_master_ref[...] = new_master
    half = params_a_ref.shape[0]
    params_a_ref[...] = new_master[:half].astype(jnp.bfloat16)
    params_b_ref[...] = jnp.broadcast_to(
        new_master[half:].astype(jnp.bfloat16)[None], params_b_ref.shape
    )


def updated(everyone, members, master, first, second):
    rows, width = master.shape
    whole = jax.ShapeDtypeStruct((rows, width), jnp.float32)
    part_a = jax.ShapeDtypeStruct((ROWS_A, width), jnp.bfloat16)
    part_b = jax.ShapeDtypeStruct((8, rows - ROWS_A, width), jnp.bfloat16)
    return pl.pallas_call(
        update_kernel,
        in_specs=in_vmem(5),
        out_specs=in_vmem(5),
        out_shape=[whole, whole, whole, part_a, part_b],
        name="updated",
    )(everyone, members, master, first, second)


def place_kernel(size_a, order, *refs):
    pieces, out, sems = refs[: len(order)], refs[-2], refs[-1]
    core, x_place = lax.axis_index("core"), lax.axis_index("x")
    copies = []
    for piece, (colour, side, step) in zip(pieces, order):
        owner = core if side == 0 else 1 - core
        if colour == 0:
            for up in range(4):
                x = lax.rem(x_place + up, 4)
                for owner in range(2):
                    source = piece.at[:, owner, up]
                    copies.append((source, out.at[x, :, owner, pl.ds(0, size_a)]))
        else:
            x = lax.rem(x_place + step, 4)
            rows = piece.shape[1]
            copies.append((piece, out.at[x, :, owner, pl.ds(size_a, rows)]))
    started = [
        pltpu.make_async_copy(source, target, sems.at[index])
        for index, (source, target) in enumerate(copies)
    ]
    for copy in started:
        copy.start()
    for copy in started:
        copy.wait()


def placed(out, pieces, order, shape, size_a):
    first = out is None
    return pl.pallas_call(
        functools.partial(place_kernel, size_a, order),
        in_specs=in_vmem(len(pieces)) + ([] if first else [pl.BlockSpec(memory_space=pl.ANY)]),
        out_specs=pl.BlockSpec(memory_space=pl.ANY),
        out_shape=jax.ShapeDtypeStruct(shape, jnp.bfloat16),
        scratch_shapes=[pltpu.SemaphoreType.DMA((8,))],
        input_output_aliases={} if first else {len(pieces): 0},
        compiler_params=pltpu.CompilerParams(vmem_limit_bytes=32 * 1024 * 1024),
        name="placed",
    )(*pieces, *([] if first else [out]))


def gathered(params_a, column_rows):
    rows_a, width = params_a.shape
    rows_b = column_rows.shape[1]
    line = jnp.concatenate(neighbours(params_a, "x"), axis=0)
    line, column_rows = lax.optimization_barrier((line, column_rows))
    own_a = lax.all_gather(line, ("z", "core"), axis=0, tiled=True)
    own_a = own_a.reshape(8, 2, 4, rows_a, width)
    column = lax.all_to_all(column_rows, "z", 0, 0)
    own_b = neighbours(column, "x")
    other_b = [shifted(piece, "core", 1) for piece in own_b]
    order = [(1, side, step) for side in range(2) for step in range(4)]
    shape = (4, 8, 2, rows_a + rows_b, width)
    out = placed(None, [*own_b, *other_b], order, shape, rows_a)
    own_a, out = lax.optimization_barrier((own_a, out))
    out = placed(out, [own_a], [(0, 0, 0)], shape, rows_a)
    return out.reshape(-1, width)


def local(activations, output_grads, master, first_moment, second_moment):
    width = activations.shape[1]
    rows = master.shape[0]
    half = rows // 2
    x_place = lax.axis_index("x")

    def product(grad_columns, act_rows):
        return lax.dot_general(
            grad_columns, act_rows, contract_first, preferred_element_type=jnp.float32
        )

    def pair_up_parts(own, given):
        return jnp.concatenate([own, shifted(given, "core", 1)], axis=0)

    def pair_up(own):
        return pair_up_parts(own, own)

    with jax.named_scope("core_swap"):
        near_acts = neighbours(activations, "x")
        kept_b, given_b = split_columns(output_grads, rows, "B")
        own_acts = pair_up(activations)
        grads_b = pair_up_parts(kept_b, given_b)
        kept_a, given_a = split_columns(output_grads, rows, "A")
        given_a, own_acts, near_acts[1], near_acts[3] = lax.optimization_barrier(
            (given_a, own_acts, near_acts[1], near_acts[3])
        )
        grads_a = pair_up_parts(kept_a, given_a)
        line_acts = [own_acts] + [pair_up(part) for part in near_acts[1:]]
    with jax.named_scope("reduce_b"):
        sums_b = lax.psum_scatter(
            product(grads_b, own_acts), "z", scatter_dimension=0, tiled=True
        )
        chunk_b = by_place(sums_b.reshape(4, half, width), "x", (lax.axis_index("z") & 1) ^ 1)
        chunks_b = [chunk_b(step) for step in range(4)]
    with jax.named_scope("reduce_a"):
        strip = 8 * half

        def columns_of(step):
            return lax.dynamic_slice_in_dim(grads_a, (x_place + step) % 4 * strip, strip, 1)

        line_grads = [
            columns_of(0),
            shifted(columns_of(3), "x", -1),
            shifted(columns_of(2), "x", 2),
            shifted(columns_of(1), "x", 1),
        ]
        sums_a = sum(product(part, acts) for part, acts in zip(line_grads, line_acts))

        exchanged_b = []

        def start_b(send_up, send_down):
            send_up, send_down, *chunks = lax.optimization_barrier(
                (send_up, send_down, *chunks_b[1:])
            )
            with jax.named_scope("reduce_b2"):
                near = shifted(chunks[2], "x", -1) + shifted(chunks[0], "x", 1)
                exchanged_b.append(chunks_b[0] + (near + shifted(chunks[1], "x", 2)))
            return send_up, send_down

        gates = {2: start_b}
        grad_a = ring_reduce(by_place(sums_a.reshape(8, half, width), "z", x_place & 1), "z", gates)
    with jax.named_scope("members"):
        members, row = gram_rows(neighbours(grad_a, "rep"), neighbours(exchanged_b.pop(), "rep"))
    with jax.named_scope("gram"):
        everyone = lax.all_to_all(row, GROUP, 0, 0)
    with jax.named_scope("adamw"):
        new_master, new_first, new_second, params_a, params_b = updated(
            everyone, members, master, first_moment, second_moment
        )
    with jax.named_scope("params"):
        params = gathered(params_a, params_b)
    return (new_master, new_first, new_second, params)


def solution(mesh):
    fine = Mesh(mesh.devices.reshape(4, 4, 8, 2), ("rep",) + GROUP)
    everyone = P(("rep",) + GROUP, None)
    block = P(GROUP, None)
    return jax.shard_map(
        local,
        mesh=fine,
        in_specs=(everyone, everyone, block, block, block),
        out_specs=(block, block, block, P()),
        check_vma=False,
    )
```
